1024 devices in a mesh: energy: 64 (over z_lo, y), mom: 16 (over z_hi, x, core).
Axes of the slice: x: 4, y: 4, z: 32 (z_hi: 2, z_lo: 16; z = z_hi * 16 + z_lo), core: 2. Of those that a mesh axis runs over, the one named last changes fastest.
Arguments:
- green_blocks: bfloat16 [2, 64, 16, 64, 64, 128], P(None, 'energy', 'mom'), may hold values from -6 to 6
- bond_grad: bfloat16 [64, 4, 64, 64], replicated, may hold values from -0.5 to 0.5
- neighbours: int32 [64, 4], replicated, may hold values from 0 to 63
- occupation: float32 [4], replicated, may hold values from 0.05 to 1
- energy_shift: int32 [4], replicated, may hold values from 1 to 16, as said below
- mom_weight: float32 [16, 3], P('mom'), may hold values from 0.3 to 1
Outputs:
- broadening: bfloat16 [64, 16, 64, 64, 128], P(None, 'mom', 'energy')
The draws below stay inside these ranges and needn't reach their ends.
Inputs may be any that keep to these rules, and one draw needn't show every extreme that they name: `energy_shift`: energy offsets of at least one point; the largest equals 16. `neighbours`: atom indices; repeats possible.
All inputs are finite; a program needn't handle non-finite values.
Results may differ from the reference program's by a relative error of at most 0.0064.
Values may be sent and summed in bfloat16 or wider, within the bound.
No kernel may reach another device: no remote copies, remote signals or barrier semaphores. Data moves between devices by JAX's collectives and lax.ppermute only.
A program may use at most 64 MiB of HBM per device.

```python
import math
import jax
import jax.numpy as jnp
from jax import lax

NO = 64
NB = 4
MODES = 4
ENERGIES = 64
ATOMS = 64
MOMENTA = 16


def draw_energy_shift(key, part):
    furthest = ENERGIES // 4
    first_key, second_key = jax.random.split(key)
    offsets = jax.random.randint(first_key, (MODES,), 1, furthest + 1)
    chosen = jax.random.randint(second_key, (), 0, MODES)
    return jnp.where(jnp.arange(MODES) == chosen, furthest, offsets).astype(jnp.int32)


def touch_ends(values, own_key, least, largest):
    extent = values.shape
    index_at = [jax.random.randint(jax.random.fold_in(own_key, axis), (), 0, extent[axis]) for axis in range(len(extent))]
    values = values.at[tuple(index_at)].set(least)
    longest = extent.index(max(extent))
    index_at[longest] = (index_at[longest] + 1) % extent[longest]
    return values.at[tuple(index_at)].set(largest)


def shard_levels(key, shape, shards, smallest, top_value):
    level, own = 1.0, jax.random.fold_in(key, 6)
    for axis_at, shards_of in shards:
        steps = jnp.exp(jax.random.uniform(jax.random.fold_in(own, axis_at), (shards_of,), jnp.float32, smallest / len(shards), top_value / len(shards)))
        level = level * jnp.repeat(steps, shape[axis_at] // shards_of).reshape([-1 if axis == axis_at else 1 for axis in range(len(shape))])
    return level


def gaussian(rng, shape, deviation, limit, pieces=(), held_as=jnp.bfloat16):
    level = shard_levels(rng, shape, pieces, -0.22, 0.18) if pieces else 1.0
    values = jax.random.normal(rng, shape, jnp.float32) * deviation * level
    return jnp.minimum(jnp.maximum(values, -limit), limit).astype(held_as)


def setup_inputs(seed: int = 0) -> dict:
    arg_keys = jax.random.split(jax.random.key(seed), 7)
    return {
        "green_blocks": gaussian(arg_keys[0], (2, ENERGIES, MOMENTA, ATOMS, NO, 2 * NO), 1.0, 6.0, ((1, 64), (2, 16))),
        "bond_grad": gaussian(arg_keys[1], (ATOMS, NB, NO, NO), (2 * NO) ** -0.5, 0.5),
        "neighbours": touch_ends(jax.random.randint(arg_keys[2], (ATOMS, NB), 0, ATOMS), jax.random.fold_in(arg_keys[2], 1), 0, ATOMS - 1).astype(jnp.int32),
        "occupation": jnp.clip(jnp.exp(jax.random.uniform(arg_keys[3], (MODES,), jnp.float32, math.log(0.05), math.log(1.0))), 0.05, 1.0),
        "energy_shift": draw_energy_shift(jax.random.fold_in(arg_keys[6], 71), 0),
        "mom_weight": jnp.clip(jnp.exp(math.log(1.0) - 1.2039728 * jax.random.uniform(arg_keys[5], (MOMENTA, 3), jnp.float32) ** shard_levels(arg_keys[5], (MOMENTA, 3), ((0, 16),), -0.2, 0.2)), 0.3, 1.0),
    }


def sandwich(blocks, bond_grad, neighbours):
    summed = jnp.zeros(blocks.shape, jnp.float32)
    for neighbour_slot in range(NB):
        picked = jnp.take(blocks, neighbours[:, neighbour_slot], axis=-3).astype(jnp.float32)
        gradient = bond_grad[:, neighbour_slot].astype(jnp.float32)
        left_product = jnp.einsum('ami,...aic->...amc', gradient, picked).astype(jnp.bfloat16)
        left_product = lax.optimization_barrier(left_product).astype(jnp.float32)
        halves = left_product.reshape(left_product.shape[:-1] + (2, NO))
        sandwiched = jnp.einsum('...amhi,aji->...amhj', halves, gradient)
        summed = summed + sandwiched.reshape(left_product.shape)
    return summed.astype(jnp.bfloat16)


def energy_mix(mixed, occupation, energy_shift):
    energies = mixed.shape[1]
    furthest = energies // 4
    widths = [(0, 0)] * mixed.ndim
    widths[1] = (furthest, furthest)
    padded = jnp.pad(mixed, widths)
    greater = jnp.zeros(mixed.shape[1:], jnp.float32)
    lesser = jnp.zeros(mixed.shape[1:], jnp.float32)
    for phonon in range(occupation.shape[0]):
        offset = energy_shift[phonon].astype(jnp.int32)
        filled = occupation[phonon]
        shifted_down = lax.dynamic_slice_in_dim(padded, (furthest - offset).astype(jnp.int32), energies, axis=1).astype(jnp.float32)
        shifted_up = lax.dynamic_slice_in_dim(padded, (furthest + offset).astype(jnp.int32), energies, axis=1).astype(jnp.float32)
        lesser = lesser + filled * shifted_down[0] + (filled + 1.0) * shifted_up[0]
        greater = greater + (filled + 1.0) * shifted_down[1] + filled * shifted_up[1]
    return (greater - lesser).astype(jnp.bfloat16)


def reference(green_blocks, bond_grad, neighbours, occupation, energy_shift, mom_weight):
    weights = [mom_weight[:, column].astype(jnp.float32).reshape(1, -1, 1, 1, 1) for column in range(3)]

    def per_energy(blocks):
        local_part = sandwich(blocks, bond_grad, neighbours)
        from_below = jnp.roll(local_part, 1, axis=1).astype(jnp.float32)
        from_above = jnp.roll(local_part, -1, axis=1).astype(jnp.float32)
        mixed = weights[0] * from_below + weights[1] * local_part.astype(jnp.float32) + weights[2] * from_above
        return mixed.astype(jnp.bfloat16)

    mixed = lax.map(per_energy, jnp.moveaxis(green_blocks, 1, 0))
    mixed = jnp.transpose(mixed, (2, 1, 0, 3, 4, 5))

    def per_momentum(slab):
        return energy_mix(slab, occupation, energy_shift)

    result = lax.map(per_momentum, mixed)
    return jnp.moveaxis(result, 0, 1)
```

```python
import functools

import jax
import jax.numpy as jnp
from jax import lax
from jax.experimental import pallas as pl
from jax.experimental.pallas import tpu as pltpu
from jax.sharding import PartitionSpec as P

CHUNKS = 1
ATOMS_PER_STEP = 8
FURTHEST = 16


def sandwich_kernel(slots, neighbours_ref, green_ref, bond_ref, *rest):
    out_refs, stacked = rest[:-1], rest[-1]
    per_step, orbitals = bond_ref.shape[0], bond_ref.shape[-1]
    group = pl.program_id(0)
    rows = orbitals // len(out_refs)
    for local in range(per_step):
        atom = group * per_step + local
        lefts = []
        for slot in range(slots):
            source = neighbours_ref[atom * slots + slot]
            blocks = jnp.concatenate([green_ref[0, source], green_ref[1, source]], axis=1)
            lefts.append(
                jnp.dot(
                    bond_ref[local, slot], blocks, preferred_element_type=jnp.float32
                ).astype(jnp.bfloat16)
            )
        buffer = stacked.at[local % 2]
        for part in range(4):
            columns = slice(part * orbitals, (part + 1) * orbitals)
            for pair in range(slots // 2):
                buffer[columns, 2 * pair * orbitals : 2 * (pair + 1) * orbitals] = jnp.concatenate(
                    [lefts[2 * pair][:, columns], lefts[2 * pair + 1][:, columns]], axis=1
                )
        gradient = jnp.concatenate([bond_ref[local, slot] for slot in range(slots)], axis=1)
        total = lax.dot_general(
            buffer[...],
            gradient,
            (((1,), (1,)), ((), ())),
            preferred_element_type=jnp.float32,
        ).astype(jnp.bfloat16)
        for kind in range(2):
            start = 2 * kind * orbitals
            both = jnp.concatenate(
                [total[start : start + orbitals], total[start + orbitals : start + 2 * orbitals]],
                axis=1,
            )
            for chunk, out_ref in enumerate(out_refs):
                out_ref[local, kind] = both[chunk * rows : (chunk + 1) * rows]


def sandwich(green, bond_grad, neighbours, chunks):
    kinds, atoms, orbitals, width = green.shape
    slots = bond_grad.shape[1]
    rows = orbitals // chunks
    per_step = ATOMS_PER_STEP
    block = pl.BlockSpec((per_step, kinds, rows, width), lambda i, n: (i, 0, 0, 0))
    return pl.pallas_call(
        functools.partial(sandwich_kernel, slots),
        grid_spec=pltpu.PrefetchScalarGridSpec(
            num_scalar_prefetch=1,
            grid=(atoms // per_step,),
            in_specs=[
                pl.BlockSpec((kinds, atoms, orbitals, width), lambda i, n: (0, 0, 0, 0)),
                pl.BlockSpec((per_step, slots, orbitals, orbitals), lambda i, n: (i, 0, 0, 0)),
            ],
            out_specs=[block] * chunks,
            scratch_shapes=[pltpu.VMEM((2, 4 * orbitals, slots * orbitals), jnp.bfloat16)],
        ),
        out_shape=[jax.ShapeDtypeStruct((atoms, kinds, rows, width), jnp.bfloat16)] * chunks,
        compiler_params=pltpu.CompilerParams(vmem_limit_bytes=32 << 20),
        name="sandwich",
    )(neighbours.reshape(-1), green, bond_grad)


def energy_kernel(modes, per_step, shift_ref, occupation_ref, moved_ref, out_ref, padded):
    energies, kinds, rows, width = moved_ref.shape
    step = pl.program_id(0)

    @pl.when(step == 0)
    def _():
        zeros = jnp.zeros((FURTHEST, kinds, rows, width), jnp.bfloat16)
        padded[pl.ds(0, FURTHEST)] = zeros
        padded[pl.ds(FURTHEST + energies, FURTHEST)] = zeros
        padded[pl.ds(FURTHEST, energies)] = moved_ref[...]

    @pl.loop(0, per_step)
    def _(local):
        centre = step * per_step + local + FURTHEST
        total = jnp.zeros((rows, width), jnp.float32)
        for mode in range(modes):
            filled = occupation_ref[mode]
            down = padded[centre - shift_ref[mode]].astype(jnp.float32)
            up = padded[centre + shift_ref[mode]].astype(jnp.float32)
            total = total + (filled + 1.0) * (down[1] - up[0]) + filled * (up[1] - down[0])
        out_ref[local] = total.astype(jnp.bfloat16)


def energy_mix(moved, occupation, energy_shift):
    energies, kinds, rows, width = moved.shape
    per_step = 8
    return pl.pallas_call(
        functools.partial(energy_kernel, occupation.shape[0], per_step),
        grid_spec=pltpu.PrefetchScalarGridSpec(
            num_scalar_prefetch=2,
            grid=(energies // per_step,),
            in_specs=[
                pl.BlockSpec((energies, kinds, rows, width), lambda i, s, o: (0, 0, 0, 0))
            ],
            out_specs=pl.BlockSpec((per_step, rows, width), lambda i, s, o: (i, 0, 0)),
            scratch_shapes=[
                pltpu.VMEM((energies + 2 * FURTHEST, kinds, rows, width), jnp.bfloat16)
            ],
        ),
        out_shape=jax.ShapeDtypeStruct((energies, rows, width), jnp.bfloat16),
        compiler_params=pltpu.CompilerParams(vmem_limit_bytes=32 << 20),
        name="energy_mix",
    )(energy_shift, occupation, moved)


def passed_along(value, axis, steps):
    count = lax.axis_size(axis)
    pairs = [(source, (source + steps) % count) for source in range(count)]
    return lax.ppermute(value, axis, pairs)


def combine(from_below, own, from_above, weights):
    mixed = weights[0, 0] * from_below.astype(jnp.float32) + weights[0, 1] * own.astype(jnp.float32)
    return (mixed + weights[0, 2] * from_above.astype(jnp.float32)).astype(jnp.bfloat16)


def on_device(green_blocks, bond_grad, neighbours, occupation, energy_shift, mom_weight):
    green = green_blocks[:, 0, 0]
    local_parts = sandwich(green, bond_grad, neighbours, CHUNKS)
    outs = []
    for part in local_parts:
        moved = lax.all_to_all(part, "energy", split_axis=0, concat_axis=0, tiled=True)
        own = energy_mix(moved, occupation, energy_shift)
        below = passed_along(own, "mom", 1)
        above = passed_along(own, "mom", -1)
        outs.append(combine(below, own, above, mom_weight))
    result = outs[0] if CHUNKS == 1 else jnp.concatenate(outs, axis=1)
    return result[:, None, None]


def solution(mesh):
    in_specs = (P(None, "energy", "mom", None, None, None), P(), P(), P(), P(), P("mom", None))
    out_specs = P(None, "mom", "energy", None, None)
    return jax.shard_map(
        on_device, mesh=mesh, in_specs=in_specs, out_specs=out_specs, check_vma=False
    )
```

```python
import functools

import jax
import jax.numpy as jnp
from jax import lax
from jax.experimental import pallas as pl
from jax.experimental.pallas import tpu as pltpu
from jax.sharding import PartitionSpec as P


ATOMS_PER_STEP = 8
ENERGIES_PER_STEP = 4
HEAD = 32


def sandwich_kernel(slots, neighbours_ref, green_ref, bond_ref, out_ref, stacked):
    per_step, orbitals = bond_ref.shape[0], bond_ref.shape[-1]
    group = pl.program_id(0)
    for local in range(per_step):
        atom = group * per_step + local
        lefts = []
        for slot in range(slots):
            source = neighbours_ref[slot, atom]
            blocks = jnp.concatenate([green_ref[0, source], green_ref[1, source]], axis=1)
            lefts.append(
                jnp.dot(
                    bond_ref[local, slot], blocks, preferred_element_type=jnp.float32
                ).astype(jnp.bfloat16)
            )
        buffer = stacked.at[local % 2]
        for part in range(4):
            columns = slice(part * orbitals, (part + 1) * orbitals)
            for pair in range(slots // 2):
                buffer[columns, 2 * pair * orbitals : 2 * (pair + 1) * orbitals] = jnp.concatenate(
                    [lefts[2 * pair][:, columns], lefts[2 * pair + 1][:, columns]], axis=1
                )
        gradient = jnp.concatenate([bond_ref[local, slot] for slot in range(slots)], axis=1)
        total = lax.dot_general(
            buffer[...],
            gradient,
            (((1,), (1,)), ((), ())),
            preferred_element_type=jnp.float32,
        ).astype(jnp.bfloat16)
        for kind in range(2):
            start = 2 * kind * orbitals
            out_ref[local, kind] = jnp.concatenate(
                [total[start : start + orbitals], total[start + orbitals : start + 2 * orbitals]],
                axis=1,
            )


def sandwich(green, bond_grad, neighbours):
    kinds, atoms, orbitals, width = green.shape
    slots = bond_grad.shape[1]
    per_step = ATOMS_PER_STEP
    block = pl.BlockSpec((per_step, kinds, orbitals, width), lambda i, n: (i, 0, 0, 0))
    return pl.pallas_call(
        functools.partial(sandwich_kernel, slots),
        grid_spec=pltpu.PrefetchScalarGridSpec(
            num_scalar_prefetch=1,
            grid=(atoms // per_step,),
            in_specs=[
                pl.BlockSpec(
                    (kinds, atoms, orbitals, width),
                    lambda i, n: (0, 0, 0, 0),
                    pipeline_mode=pl.Buffered(1),
                ),
                pl.BlockSpec((per_step, slots, orbitals, orbitals), lambda i, n: (i, 0, 0, 0)),
            ],
            out_specs=block,
            scratch_shapes=[pltpu.VMEM((2, 4 * orbitals, slots * orbitals), jnp.bfloat16)],
        ),
        out_shape=jax.ShapeDtypeStruct((atoms, kinds, orbitals, width), jnp.bfloat16),
        compiler_params=pltpu.CompilerParams(vmem_limit_bytes=60 << 20),
        name="sandwich",
    )(neighbours.T, green, bond_grad)


def energy_kernel(modes, first, per_step, energies, shift_ref, occupation_ref, moved_ref, out_ref):
    _, _, rows, width = moved_ref.shape
    start = first + pl.program_id(0) * per_step
    for local in range(per_step):
        energy = start + local
        total = jnp.zeros((rows, width), jnp.float32)
        for mode in range(modes):
            shift = shift_ref[mode]
            filled = occupation_ref[mode]
            below, above = energy - shift, energy + shift
            down_on = jnp.where(below >= 0, 1.0, 0.0)
            up_on = jnp.where(above < energies, 1.0, 0.0)
            down = moved_ref[jnp.maximum(below, 0)].astype(jnp.float32)
            up = moved_ref[jnp.minimum(above, energies - 1)].astype(jnp.float32)
            total = total + ((filled + 1.0) * down_on) * down[1] - (filled * down_on) * down[0]
            total = total + (filled * up_on) * up[1] - ((filled + 1.0) * up_on) * up[0]
        out_ref[local] = total.astype(jnp.bfloat16)


def energy_mix(moved, occupation, energy_shift, first, count):
    energies, kinds, rows, width = moved.shape
    per_step = ENERGIES_PER_STEP
    return pl.pallas_call(
        functools.partial(energy_kernel, occupation.shape[0], first, per_step, energies),
        grid_spec=pltpu.PrefetchScalarGridSpec(
            num_scalar_prefetch=2,
            grid=(count // per_step,),
            in_specs=[
                pl.BlockSpec((energies, kinds, rows, width), lambda i, s, o: (0, 0, 0, 0))
            ],
            out_specs=pl.BlockSpec((per_step, rows, width), lambda i, s, o: (i, 0, 0)),
        ),
        out_shape=jax.ShapeDtypeStruct((count, rows, width), jnp.bfloat16),
        compiler_params=pltpu.CompilerParams(vmem_limit_bytes=32 << 20),
        cost_estimate=pl.CostEstimate(
            flops=32 * count * rows * width, bytes_accessed=6 << 20, transcendentals=0
        ),
        name="energy_mix",
    )(energy_shift, occupation, moved)


def partial_kernel(weight_ref, own_ref, core_ref, out_ref):
    own_weight, core_weight = weight_ref[0], weight_ref[1]

    @pl.loop(0, own_ref.shape[0])
    def _(energy):
        out_ref[energy] = own_weight * own_ref[energy].astype(jnp.float32) + core_weight * (
            core_ref[energy].astype(jnp.float32)
        )


def partial_mix(weights, own, core):
    vmem = pl.BlockSpec(memory_space=pltpu.VMEM)
    return pl.pallas_call(
        partial_kernel,
        in_specs=[pl.BlockSpec(memory_space=pltpu.SMEM), vmem, vmem],
        out_specs=vmem,
        out_shape=jax.ShapeDtypeStruct(own.shape, jnp.float32),
        compiler_params=pltpu.CompilerParams(vmem_limit_bytes=16 << 20),
        name="partial_mix",
    )(weights, own, core)


def combine_kernel(weight_ref, partial_a, partial_b, far_a, far_b, relayed_b, out_ref):
    far_weight = weight_ref[2]
    head = partial_a.shape[0]

    @pl.loop(0, head)
    def _(energy):
        far = far_a[energy].astype(jnp.float32)
        out_ref[energy] = (partial_a[energy] + far_weight * far).astype(jnp.bfloat16)

    @pl.loop(0, partial_b.shape[0])
    def _(energy):
        far = far_b[energy].astype(jnp.float32) + relayed_b[energy].astype(jnp.float32)
        out_ref[head + energy] = (partial_b[energy] + far_weight * far).astype(jnp.bfloat16)


def combine(weights, partial_a, partial_b, far_a, far_b, relayed_b):
    vmem = pl.BlockSpec(memory_space=pltpu.VMEM)
    (head, rows, width), tail = partial_a.shape, partial_b.shape[0]
    return pl.pallas_call(
        combine_kernel,
        in_specs=[pl.BlockSpec(memory_space=pltpu.SMEM)] + [vmem] * 5,
        out_specs=vmem,
        out_shape=jax.ShapeDtypeStruct((head + tail, rows, width), jnp.bfloat16),
        compiler_params=pltpu.CompilerParams(vmem_limit_bytes=16 << 20),
        name="combine",
    )(weights, partial_a, partial_b, far_a, far_b, relayed_b)


def swaps(pairs):
    return [move for one, other in pairs for move in ((one, other), (other, one))]


def exchange(own_a, own_b):
    count = lax.axis_size("mom")
    half = count // 2
    on_chip = swaps([(k, k + 1) for k in range(0, count, 2)])
    far = [(k, (k + 1) % count) for k in range(1, count, 2)]
    long = [(half - 1, half), (count - 1, 0)]
    near = [pair for pair in far if pair not in long]
    helper = {half - 1: half - 3, half: half + 2, count - 1: count - 3, 0: 2}
    out = list(helper.items())
    across = [(helper[one], other) for one, other in swaps(long)]
    relay = lax.ppermute(own_b, "mom", out)
    far_a = lax.ppermute(own_a, "mom", swaps(far))
    relayed_b = lax.ppermute(relay, "mom", across)
    far_b = lax.ppermute(own_b, "mom", swaps(near))
    core_a = lax.ppermute(own_a, "mom", on_chip)
    core_b = lax.ppermute(own_b, "mom", on_chip)
    return core_a, core_b, far_a, far_b, relayed_b


def on_device(green_blocks, bond_grad, neighbours, occupation, energy_shift, mom_weight):
    local_part = sandwich(green_blocks[:, 0, 0], bond_grad, neighbours)
    moved = lax.all_to_all(local_part, "energy", split_axis=0, concat_axis=0, tiled=True)
    own_b = energy_mix(moved, occupation, energy_shift, HEAD, moved.shape[0] - HEAD)
    own_a = energy_mix(moved, occupation, energy_shift, 0, HEAD)
    even = lax.axis_index("mom") % 2 == 0
    core_weight = jnp.where(even, mom_weight[0, 2], mom_weight[0, 0])
    far_weight = jnp.where(even, mom_weight[0, 0], mom_weight[0, 2])
    weights = jnp.stack([mom_weight[0, 1], core_weight, far_weight])
    core_a, core_b, far_a, far_b, relayed_b = exchange(own_a, own_b)
    partial_a = partial_mix(weights, own_a, core_a)
    partial_b = partial_mix(weights, own_b, core_b)
    return combine(weights, partial_a, partial_b, far_a, far_b, relayed_b)[:, None, None]


def solution(mesh):
    in_specs = (P(None, "energy", "mom", None, None, None), P(), P(), P(), P(), P("mom", None))
    out_specs = P(None, "mom", "energy", None, None)

    return jax.shard_map(
        on_device, mesh=mesh, in_specs=in_specs, out_specs=out_specs, check_vma=False
    )
```

```python
import functools

import jax
import jax.numpy as jnp
from jax import lax
from jax.experimental import pallas as pl
from jax.experimental.pallas import tpu as pltpu
from jax.sharding import PartitionSpec as P


ATOMS_PER_STEP = 16
ENERGIES_PER_STEP = 4
HEAD = 28


def sandwich_kernel(slots, neighbours_ref, green_ref, bond_ref, out_ref, stacked):
    per_step, orbitals = bond_ref.shape[0], bond_ref.shape[-1]
    group = pl.program_id(0)
    for local in range(per_step):
        atom = group * per_step + local
        lefts = []
        for slot in range(slots):
            source = neighbours_ref[slot, atom]
            blocks = jnp.concatenate([green_ref[0, source], green_ref[1, source]], axis=1)
            lefts.append(
                jnp.dot(
                    bond_ref[local, slot], blocks, preferred_element_type=jnp.float32
                ).astype(jnp.bfloat16)
            )
        buffer = stacked.at[local]
        for part in range(4):
            columns = slice(part * orbitals, (part + 1) * orbitals)
            for pair in range(slots // 2):
                buffer[columns, 2 * pair * orbitals : 2 * (pair + 1) * orbitals] = jnp.concatenate(
                    [lefts[2 * pair][:, columns], lefts[2 * pair + 1][:, columns]], axis=1
                )
    for local in range(per_step):
        buffer = stacked.at[local]
        gradient = jnp.concatenate([bond_ref[local, slot] for slot in range(slots)], axis=1)
        total = lax.dot_general(
            buffer[...],
            gradient,
            (((1,), (1,)), ((), ())),
            preferred_element_type=jnp.float32,
        ).astype(jnp.bfloat16)
        for kind in range(2):
            start = 2 * kind * orbitals
            out_ref[local, kind] = jnp.concatenate(
                [total[start : start + orbitals], total[start + orbitals : start + 2 * orbitals]],
                axis=1,
            )


def sandwich(green, bond_grad, neighbours):
    kinds, atoms, orbitals, width = green.shape
    slots = bond_grad.shape[1]
    per_step = ATOMS_PER_STEP
    block = pl.BlockSpec((per_step, kinds, orbitals, width), lambda i, n: (i, 0, 0, 0))
    return pl.pallas_call(
        functools.partial(sandwich_kernel, slots),
        grid_spec=pltpu.PrefetchScalarGridSpec(
            num_scalar_prefetch=1,
            grid=(atoms // per_step,),
            in_specs=[
                pl.BlockSpec(
                    (kinds, atoms, orbitals, width),
                    lambda i, n: (0, 0, 0, 0),
                    pipeline_mode=pl.Buffered(1),
                ),
                pl.BlockSpec((per_step, slots, orbitals, orbitals), lambda i, n: (i, 0, 0, 0)),
            ],
            out_specs=block,
            scratch_shapes=[pltpu.VMEM((per_step, 4 * orbitals, slots * orbitals), jnp.bfloat16)],
        ),
        out_shape=jax.ShapeDtypeStruct((atoms, kinds, orbitals, width), jnp.bfloat16),
        compiler_params=pltpu.CompilerParams(vmem_limit_bytes=60 << 20),
        name="sandwich",
    )(neighbours.T, green, bond_grad)


def energy_kernel(modes, first, per_step, energies, shift_ref, occupation_ref, moved_ref, out_ref):
    _, _, rows, width = moved_ref.shape
    start = first + pl.program_id(0) * per_step
    for local in range(per_step):
        energy = start + local
        total = jnp.zeros((rows, width), jnp.float32)
        for mode in range(modes):
            shift = shift_ref[mode]
            filled = occupation_ref[mode]
            below, above = energy - shift, energy + shift
            down_on = jnp.where(below >= 0, 1.0, 0.0)
            up_on = jnp.where(above < energies, 1.0, 0.0)
            down = moved_ref[jnp.maximum(below, 0)].astype(jnp.float32)
            up = moved_ref[jnp.minimum(above, energies - 1)].astype(jnp.float32)
            total = total + ((filled + 1.0) * down_on) * down[1] - (filled * down_on) * down[0]
            total = total + (filled * up_on) * up[1] - ((filled + 1.0) * up_on) * up[0]
        out_ref[local] = total.astype(jnp.bfloat16)


def energy_mix(moved, occupation, energy_shift, first, count):
    energies, kinds, rows, width = moved.shape
    per_step = ENERGIES_PER_STEP
    return pl.pallas_call(
        functools.partial(energy_kernel, occupation.shape[0], first, per_step, energies),
        grid_spec=pltpu.PrefetchScalarGridSpec(
            num_scalar_prefetch=2,
            grid=(count // per_step,),
            in_specs=[
                pl.BlockSpec((energies, kinds, rows, width), lambda i, s, o: (0, 0, 0, 0))
            ],
            out_specs=pl.BlockSpec((per_step, rows, width), lambda i, s, o: (i, 0, 0)),
        ),
        out_shape=jax.ShapeDtypeStruct((count, rows, width), jnp.bfloat16),
        compiler_params=pltpu.CompilerParams(vmem_limit_bytes=32 << 20),
        cost_estimate=pl.CostEstimate(
            flops=32 * count * rows * width, bytes_accessed=6 << 20, transcendentals=0
        ),
        name="energy_mix",
    )(energy_shift, occupation, moved)


def partial_kernel(weight_ref, own_ref, core_ref, out_ref):
    own_weight, core_weight = weight_ref[0], weight_ref[1]

    @pl.loop(0, own_ref.shape[0])
    def _(energy):
        out_ref[energy] = own_weight * own_ref[energy].astype(jnp.float32) + core_weight * (
            core_ref[energy].astype(jnp.float32)
        )


def partial_mix(weights, own, core):
    vmem = pl.BlockSpec(memory_space=pltpu.VMEM)
    return pl.pallas_call(
        partial_kernel,
        in_specs=[pl.BlockSpec(memory_space=pltpu.SMEM), vmem, vmem],
        out_specs=vmem,
        out_shape=jax.ShapeDtypeStruct(own.shape, jnp.float32),
        compiler_params=pltpu.CompilerParams(vmem_limit_bytes=16 << 20),
        name="partial_mix",
    )(weights, own, core)


def combine_kernel(weight_ref, partial_a, partial_b, far_a, far_b, relayed_b, out_ref):
    far_weight = weight_ref[2]
    head = partial_a.shape[0]

    @pl.loop(0, head)
    def _(energy):
        far = far_a[energy].astype(jnp.float32)
        out_ref[energy] = (partial_a[energy] + far_weight * far).astype(jnp.bfloat16)

    @pl.loop(0, partial_b.shape[0])
    def _(energy):
        far = far_b[energy].astype(jnp.float32) + relayed_b[energy].astype(jnp.float32)
        out_ref[head + energy] = (partial_b[energy] + far_weight * far).astype(jnp.bfloat16)


def combine(weights, partial_a, partial_b, far_a, far_b, relayed_b):
    vmem = pl.BlockSpec(memory_space=pltpu.VMEM)
    (head, rows, width), tail = partial_a.shape, partial_b.shape[0]
    return pl.pallas_call(
        combine_kernel,
        in_specs=[pl.BlockSpec(memory_space=pltpu.SMEM)] + [vmem] * 5,
        out_specs=vmem,
        out_shape=jax.ShapeDtypeStruct((head + tail, rows, width), jnp.bfloat16),
        compiler_params=pltpu.CompilerParams(vmem_limit_bytes=16 << 20),
        name="combine",
    )(weights, partial_a, partial_b, far_a, far_b, relayed_b)


def swaps(pairs):
    return [move for one, other in pairs for move in ((one, other), (other, one))]


def exchange(own_a, own_b):
    count = lax.axis_size("mom")
    half = count // 2
    on_chip = swaps([(k, k + 1) for k in range(0, count, 2)])
    far = [(k, (k + 1) % count) for k in range(1, count, 2)]
    long = [(half - 1, half), (count - 1, 0)]
    near = [pair for pair in far if pair not in long]
    helper = {half - 1: half - 3, half: half + 2, count - 1: count - 3, 0: 2}
    out = list(helper.items())
    across = [(helper[one], other) for one, other in swaps(long)]
    relay = lax.ppermute(own_b, "mom", out)
    far_a = lax.ppermute(own_a, "mom", swaps(far))
    relayed_b = lax.ppermute(relay, "mom", across)
    far_b = lax.ppermute(own_b, "mom", swaps(near))
    core_a = lax.ppermute(own_a, "mom", on_chip)
    core_b = lax.ppermute(own_b, "mom", on_chip)
    return core_a, core_b, far_a, far_b, relayed_b


def on_device(green_blocks, bond_grad, neighbours, occupation, energy_shift, mom_weight):
    local_part = sandwich(green_blocks[:, 0, 0], bond_grad, neighbours)
    moved = lax.all_to_all(local_part, "energy", split_axis=0, concat_axis=0, tiled=True)
    own_b = energy_mix(moved, occupation, energy_shift, HEAD, moved.shape[0] - HEAD)
    own_a = energy_mix(moved, occupation, energy_shift, 0, HEAD)
    even = lax.axis_index("mom") % 2 == 0
    core_weight = jnp.where(even, mom_weight[0, 2], mom_weight[0, 0])
    far_weight = jnp.where(even, mom_weight[0, 0], mom_weight[0, 2])
    weights = jnp.stack([mom_weight[0, 1], core_weight, far_weight])
    core_a, core_b, far_a, far_b, relayed_b = exchange(own_a, own_b)
    partial_a = partial_mix(weights, own_a, core_a)
    partial_b = partial_mix(weights, own_b, core_b)
    return combine(weights, partial_a, partial_b, far_a, far_b, relayed_b)[:, None, None]


def solution(mesh):
    in_specs = (P(None, "energy", "mom", None, None, None), P(), P(), P(), P(), P("mom", None))
    out_specs = P(None, "mom", "energy", None, None)

    return jax.shard_map(
        on_device, mesh=mesh, in_specs=in_specs, out_specs=out_specs, check_vma=False
    )
```

```python
import functools

import jax
import jax.numpy as jnp
from jax import lax
from jax.experimental import pallas as pl
from jax.experimental.pallas import tpu as pltpu
from jax.sharding import PartitionSpec as P


ATOMS_PER_STEP = 16
HEAD = 32


def sandwich_kernel(slots, neighbours_ref, green_ref, bond_ref, out_ref, stacked):
    per_step, orbitals = bond_ref.shape[0], bond_ref.shape[-1]
    group = pl.program_id(0)
    for local in range(per_step):
        atom = group * per_step + local
        lefts = []
        for slot in range(slots):
            source = neighbours_ref[slot, atom]
            blocks = jnp.concatenate([green_ref[0, source], green_ref[1, source]], axis=1)
            lefts.append(
                jnp.dot(
                    bond_ref[local, slot], blocks, preferred_element_type=jnp.float32
                ).astype(jnp.bfloat16)
            )
        buffer = stacked.at[local]
        for part in range(4):
            columns = slice(part * orbitals, (part + 1) * orbitals)
            for pair in range(slots // 2):
                buffer[columns, 2 * pair * orbitals : 2 * (pair + 1) * orbitals] = jnp.concatenate(
                    [lefts[2 * pair][:, columns], lefts[2 * pair + 1][:, columns]], axis=1
                )
    for local in range(per_step):
        buffer = stacked.at[local]
        gradient = jnp.concatenate([bond_ref[local, slot] for slot in range(slots)], axis=1)
        total = lax.dot_general(
            buffer[...],
            gradient,
            (((1,), (1,)), ((), ())),
            preferred_element_type=jnp.float32,
        ).astype(jnp.bfloat16)
        for kind in range(2):
            start = 2 * kind * orbitals
            out_ref[local, kind] = jnp.concatenate(
                [total[start : start + orbitals], total[start + orbitals : start + 2 * orbitals]],
                axis=1,
            )


def sandwich(green, bond_grad, neighbours):
    kinds, atoms, orbitals, width = green.shape
    slots = bond_grad.shape[1]
    per_step = ATOMS_PER_STEP
    block = pl.BlockSpec((per_step, kinds, orbitals, width), lambda i, n: (i, 0, 0, 0))
    return pl.pallas_call(
        functools.partial(sandwich_kernel, slots),
        grid_spec=pltpu.PrefetchScalarGridSpec(
            num_scalar_prefetch=1,
            grid=(atoms // per_step,),
            in_specs=[
                pl.BlockSpec(
                    (kinds, atoms, orbitals, width),
                    lambda i, n: (0, 0, 0, 0),
                    pipeline_mode=pl.Buffered(1),
                ),
                pl.BlockSpec((per_step, slots, orbitals, orbitals), lambda i, n: (i, 0, 0, 0)),
            ],
            out_specs=block,
            scratch_shapes=[pltpu.VMEM((per_step, 4 * orbitals, slots * orbitals), jnp.bfloat16)],
        ),
        out_shape=jax.ShapeDtypeStruct((atoms, kinds, orbitals, width), jnp.bfloat16),
        compiler_params=pltpu.CompilerParams(vmem_limit_bytes=60 << 20),
        name="sandwich",
    )(neighbours.T, green, bond_grad)


def energy_kernel(modes, first, shift_ref, occupation_ref, moved_ref, out_ref):
    energies, _, rows, width = moved_ref.shape

    @pl.loop(0, out_ref.shape[0])
    def _(local):
        energy = first + local
        total = jnp.zeros((rows, width), jnp.float32)
        for mode in range(modes):
            shift = shift_ref[mode]
            filled = occupation_ref[mode]
            below, above = energy - shift, energy + shift
            down_on = jnp.where(below >= 0, 1.0, 0.0)
            up_on = jnp.where(above < energies, 1.0, 0.0)
            down = moved_ref[jnp.maximum(below, 0)].astype(jnp.float32)
            up = moved_ref[jnp.minimum(above, energies - 1)].astype(jnp.float32)
            total = total + ((filled + 1.0) * down_on) * down[1] - (filled * down_on) * down[0]
            total = total + (filled * up_on) * up[1] - ((filled + 1.0) * up_on) * up[0]
        out_ref[local] = total.astype(jnp.bfloat16)


def energy_mix(moved, occupation, energy_shift, first, count):
    _, _, rows, width = moved.shape
    vmem, smem = pl.BlockSpec(memory_space=pltpu.VMEM), pl.BlockSpec(memory_space=pltpu.SMEM)
    return pl.pallas_call(
        functools.partial(energy_kernel, occupation.shape[0], first),
        in_specs=[smem, smem, vmem],
        out_specs=vmem,
        out_shape=jax.ShapeDtypeStruct((count, rows, width), jnp.bfloat16),
        compiler_params=pltpu.CompilerParams(vmem_limit_bytes=16 << 20),
        cost_estimate=pl.CostEstimate(
            flops=32 * count * rows * width, bytes_accessed=6 << 20, transcendentals=0
        ),
        name="energy_mix",
    )(energy_shift, occupation, moved)


def partial_kernel(weight_ref, own_ref, core_ref, out_ref):
    own_weight, core_weight = weight_ref[0], weight_ref[1]

    @pl.loop(0, own_ref.shape[0])
    def _(energy):
        out_ref[energy] = own_weight * own_ref[energy].astype(jnp.float32) + core_weight * (
            core_ref[energy].astype(jnp.float32)
        )


def partial_mix(weights, own, core):
    vmem = pl.BlockSpec(memory_space=pltpu.VMEM)
    return pl.pallas_call(
        partial_kernel,
        in_specs=[pl.BlockSpec(memory_space=pltpu.SMEM), vmem, vmem],
        out_specs=vmem,
        out_shape=jax.ShapeDtypeStruct(own.shape, jnp.float32),
        compiler_params=pltpu.CompilerParams(vmem_limit_bytes=16 << 20),
        name="partial_mix",
    )(weights, own, core)


def combine_kernel(weight_ref, partial_a, partial_b, far_a, far_b, relayed_b, out_ref):
    far_weight = weight_ref[2]
    head = partial_a.shape[0]

    @pl.loop(0, head)
    def _(energy):
        far = far_a[energy].astype(jnp.float32)
        out_ref[energy] = (partial_a[energy] + far_weight * far).astype(jnp.bfloat16)

    @pl.loop(0, partial_b.shape[0])
    def _(energy):
        far = far_b[energy].astype(jnp.float32) + relayed_b[energy].astype(jnp.float32)
        out_ref[head + energy] = (partial_b[energy] + far_weight * far).astype(jnp.bfloat16)


def combine(weights, partial_a, partial_b, far_a, far_b, relayed_b):
    vmem = pl.BlockSpec(memory_space=pltpu.VMEM)
    (head, rows, width), tail = partial_a.shape, partial_b.shape[0]
    return pl.pallas_call(
        combine_kernel,
        in_specs=[pl.BlockSpec(memory_space=pltpu.SMEM)] + [vmem] * 5,
        out_specs=vmem,
        out_shape=jax.ShapeDtypeStruct((head + tail, rows, width), jnp.bfloat16),
        compiler_params=pltpu.CompilerParams(vmem_limit_bytes=16 << 20),
        name="combine",
    )(weights, partial_a, partial_b, far_a, far_b, relayed_b)


def swaps(pairs):
    return [move for one, other in pairs for move in ((one, other), (other, one))]


def exchange(own_a, own_b):
    count = lax.axis_size("mom")
    half = count // 2
    on_chip = swaps([(k, k + 1) for k in range(0, count, 2)])
    far = [(k, (k + 1) % count) for k in range(1, count, 2)]
    long = [(half - 1, half), (count - 1, 0)]
    near = [pair for pair in far if pair not in long]
    helper = {half - 1: half - 3, half: half + 2, count - 1: count - 3, 0: 2}
    out = list(helper.items())
    across = [(helper[one], other) for one, other in swaps(long)]
    relay = lax.ppermute(own_b, "mom", out)
    far_a = lax.ppermute(own_a, "mom", swaps(far))
    relayed_b = lax.ppermute(relay, "mom", across)
    far_b = lax.ppermute(own_b, "mom", swaps(near))
    core_a = lax.ppermute(own_a, "mom", on_chip)
    core_b = lax.ppermute(own_b, "mom", on_chip)
    return core_a, core_b, far_a, far_b, relayed_b


def on_device(green_blocks, bond_grad, neighbours, occupation, energy_shift, mom_weight):
    local_part = sandwich(green_blocks[:, 0, 0], bond_grad, neighbours)
    moved = lax.all_to_all(local_part, "energy", split_axis=0, concat_axis=0, tiled=True)
    own_b = energy_mix(moved, occupation, energy_shift, HEAD, moved.shape[0] - HEAD)
    own_a = energy_mix(moved, occupation, energy_shift, 0, HEAD)
    even = lax.axis_index("mom") % 2 == 0
    core_weight = jnp.where(even, mom_weight[0, 2], mom_weight[0, 0])
    far_weight = jnp.where(even, mom_weight[0, 0], mom_weight[0, 2])
    weights = jnp.stack([mom_weight[0, 1], core_weight, far_weight])
    core_a, core_b, far_a, far_b, relayed_b = exchange(own_a, own_b)
    partial_a = partial_mix(weights, own_a, core_a)
    partial_b = partial_mix(weights, own_b, core_b)
    return combine(weights, partial_a, partial_b, far_a, far_b, relayed_b)[:, None, None]


def solution(mesh):
    in_specs = (P(None, "energy", "mom", None, None, None), P(), P(), P(), P(), P("mom", None))
    out_specs = P(None, "mom", "energy", None, None)

    return jax.shard_map(
        on_device, mesh=mesh, in_specs=in_specs, out_specs=out_specs, check_vma=False
    )
```
